32 devices in a mesh: ab: 16 (over z, y, core), ij: 2 (over x).
Axes of the slice: x: 2, y: 2, z: 4, core: 2. Of those that a mesh axis runs over, the one named last changes fastest.
Arguments:
- amplitudes: float32 [128, 2048], P('ab', 'ij'), may hold values from -6 to 6
- integrals: float32 [16384, 2048], P('ab'), may hold values from -0.125 to 0.125
- occ_pairs: float32 [128], P(('ab', 'ij')), may hold values from -2 to -0.5
- vir_pairs: float32 [16384], P('ab'), may hold values from 1 to 4
Outputs:
- update: float32 [128, 16384], P(('ab', 'ij'))
The draws below stay inside these ranges and needn't reach their ends.
All inputs are finite; a program needn't handle non-finite values.
Results may differ from the reference program's by a relative error of at most 0.00007.
Values sent between devices are 32-bit elements; how exact they have to be, the bound alone decides.
No kernel may reach another device: no remote copies, remote signals or barrier semaphores. Data moves between devices by JAX's collectives and lax.ppermute only.
A program may use at most 64 MiB of HBM per device.

```python
import jax
import jax.numpy as jnp
from jax import lax

CD = 2048
IJ = 128
AB = 16384


def steps_of(stream_key, shape, shards, smallest, largest):
    def one(position, shards_of):
        draws = jax.random.uniform(jax.random.fold_in(jax.random.fold_in(stream_key, 6), position), (shards_of,), jnp.float32, smallest / len(shards), largest / len(shards))
        return jnp.repeat(jnp.exp(draws), shape[position] // shards_of).reshape((-1,) + (1,) * (len(shape) - position - 1))

    loudness = one(*shards[0])
    for cut in shards[1:]:
        loudness = loudness * one(*cut)
    return loudness


def bell_draw(stream_key, shape, deviation, reach, shards=(), dtype=jnp.bfloat16):
    gain = steps_of(stream_key, shape, shards, -0.22, 0.18) if shards else 1.0
    values = jax.random.normal(stream_key, shape, jnp.float32) * deviation * gain
    return jnp.minimum(jnp.maximum(values, -reach), reach).astype(dtype)


def setup_inputs(seed: int = 0) -> dict:
    splits = jax.random.split(jax.random.key(seed), 5)
    return {
        "amplitudes": bell_draw(splits[0], (IJ, CD), 1.0, 6.0, ((0, 16), (1, 2)), jnp.float32),
        "integrals": bell_draw(splits[1], (AB, CD), CD ** -0.5, 0.125, ((0, 16),), jnp.float32),
        "occ_pairs": jnp.clip(-2.0 + 1.5 * jax.random.uniform(splits[2], (IJ,), jnp.float32) ** steps_of(splits[2], (IJ,), ((0, 32),), -0.2, 0.2), -2.0, -0.5),
        "vir_pairs": jnp.clip(1.0 + 3.0 * jax.random.uniform(splits[3], (AB,), jnp.float32) ** steps_of(splits[3], (AB,), ((0, 16),), -0.2, 0.2), 1.0, 4.0),
    }


def reference(amplitudes, integrals, occ_pairs, vir_pairs):
    residual = jnp.dot(amplitudes, integrals.T, precision=lax.Precision.HIGHEST, preferred_element_type=jnp.float32)
    return residual / (vir_pairs[None, :] - occ_pairs[:, None])
```

```python
import functools
import itertools

import jax
import jax.numpy as jnp
from jax import lax
from jax.experimental import pallas as pl
from jax.experimental.pallas import tpu as pltpu
from jax.sharding import Mesh, PartitionSpec as P

LANES = 128
NT = (((1,), (1,)), ((), ()))
VMEM = pl.BlockSpec(memory_space=pltpu.VMEM)


def limit(mib):
    return pltpu.CompilerParams(vmem_limit_bytes=mib * 1024 * 1024)


def is_power(n):
    return n & (n - 1) == 0


def target(i, d, n):
    return i ^ d if is_power(n) else (i + d) % n


def source(i, d, n):
    return i ^ d if is_power(n) else (i + n - d) % n


def send(x, axes, distance):
    sizes = [lax.axis_size(a) for a in axes]
    pairs = []
    for at in itertools.product(*(range(n) for n in sizes)):
        to = [target(i, d, n) for i, d, n in zip(at, distance, sizes)]
        s = t = 0
        for n, i, j in zip(sizes, at, to):
            s, t = s * n + i, t * n + j
        pairs.append((s, t))
    return lax.ppermute(x, axes, pairs)


def split(x):
    hi = x.astype(jnp.bfloat16)
    return hi, (x - hi.astype(jnp.float32)).astype(jnp.bfloat16)


def dot(a, b):
    return lax.dot_general(a, b, NT, preferred_element_type=jnp.float32)


def split_kernel(chunk, integrals_ref, hi_ref, lo_ref, landed, sems):
    starts = range(0, landed.shape[0], chunk)
    copies = [
        pltpu.make_async_copy(
            integrals_ref.at[pl.ds(start, chunk)], landed.at[pl.ds(start, chunk)], sems.at[i]
        )
        for i, start in enumerate(starts)
    ]
    for copy in copies:
        copy.start()
    for copy, start in zip(copies, starts):
        copy.wait()
        part = slice(start, start + chunk)
        hi_ref[part, :], lo_ref[part, :] = split(landed[part, :])


def split_integrals(integrals):
    panel, cols = integrals.shape
    chunk = min(128, panel)
    return pl.pallas_call(
        functools.partial(split_kernel, chunk),
        out_shape=[jax.ShapeDtypeStruct((panel, cols), jnp.bfloat16)] * 2,
        in_specs=[pl.BlockSpec(memory_space=pltpu.HBM)],
        out_specs=[VMEM] * 2,
        scratch_shapes=[
            pltpu.VMEM((panel, cols), jnp.float32),
            pltpu.SemaphoreType.DMA((panel // chunk,)),
        ],
        compiler_params=limit(42),
        cost_estimate=pl.CostEstimate(
            flops=3 * panel * cols, bytes_accessed=8 * panel * cols, transcendentals=0
        ),
        name="split_integrals",
    )(integrals)


def pack_kernel(amplitudes_ref, occ_ref, out_ref):
    slices, per, width = out_ref.shape
    cols = width - LANES
    for s in range(slices):
        out_ref[s, :, :cols] = amplitudes_ref[s * per : (s + 1) * per, :]
        for row in range(per):
            out_ref[s, row, cols:] = jnp.full((LANES,), occ_ref[row], jnp.float32)


def pack(amplitudes, occ_pairs):
    rows, cols = amplitudes.shape
    per = occ_pairs.shape[0]
    return pl.pallas_call(
        pack_kernel,
        out_shape=jax.ShapeDtypeStruct((rows // per, per, cols + LANES), jnp.float32),
        in_specs=[VMEM, pl.BlockSpec(memory_space=pltpu.SMEM)],
        out_specs=VMEM,
        name="pack",
    )(amplitudes, occ_pairs)


def sort_kernel(axis, *refs):
    *block_refs, _, out_ref = refs
    slices = out_ref.shape[0]
    me = lax.axis_index(axis)
    for d in range(slices):
        for k, ref in enumerate(block_refs):
            out_ref[d, k] = ref[target(me, d, slices)]


def sort_slices(blocks, after):
    slices, per, width = blocks[0].shape
    return pl.pallas_call(
        functools.partial(sort_kernel, "ij"),
        out_shape=jax.ShapeDtypeStruct((slices, len(blocks), per, width), jnp.float32),
        in_specs=[VMEM] * len(blocks) + [pl.BlockSpec(memory_space=pl.ANY)],
        out_specs=VMEM,
        compiler_params=limit(8),
        name="sort_slices",
    )(*blocks, after)


def contract_kernel(keys, chunk, *refs):
    *piece_refs, hi_ref, lo_ref, vir_ref, out_ref, amps = refs
    outer, inner, cores, per, panel = out_ref.shape
    slices = hi_ref.shape[1] // (piece_refs[0].shape[2] - LANES)
    cols = hi_ref.shape[1] // slices
    at = [lax.axis_index(a) for a in ("outer", "inner", "core", "ij")]
    rows = amps.shape[0] // 2
    group = outer * per
    energy = [None] * (rows // group)
    for (core, near, part), ref in zip(keys, piece_refs):
        base = (core * inner + near) * group
        hi, lo = split(ref[:, :, :cols].reshape(group, cols))
        where = pl.ds(pl.multiple_of(source(at[3], part, slices) * cols, LANES), cols)
        amps[base : base + group, where] = hi
        amps[rows + base : rows + base + group, where] = lo
        if part == 0:
            energy[base // group] = ref[:, :, cols:].reshape(group, LANES)
    energy = jnp.concatenate(energy, axis=0)[:, :1]
    for start in range(0, panel, chunk):
        some = slice(start, start + chunk)
        wide = dot(amps[...], hi_ref[some, :])
        residual = wide[:rows] + (wide[rows:] + dot(amps[:rows, :], lo_ref[some, :]))
        update = residual / (vir_ref[:, some] - energy)
        update = update.reshape(cores, inner, outer, per, chunk)
        for c, n, o in itertools.product(range(cores), range(inner), range(outer)):
            out_ref[
                source(at[0], o, outer), source(at[1], n, inner), source(at[2], c, cores), :, some
            ] = update[c, n, o]


def contract(pieces, hi, lo, vir_pairs, inner, cores):
    keys = sorted(pieces)
    outer, per, width = pieces[keys[0]].shape
    panel, cols = hi.shape
    rows = outer * inner * cores * per
    return pl.pallas_call(
        functools.partial(contract_kernel, keys, min(256, panel)),
        out_shape=jax.ShapeDtypeStruct((outer, inner, cores, per, panel), jnp.float32),
        in_specs=[VMEM] * (len(keys) + 3),
        out_specs=VMEM,
        scratch_shapes=[pltpu.VMEM((2 * rows, cols), jnp.bfloat16)],
        compiler_params=limit(32),
        cost_estimate=pl.CostEstimate(
            flops=6 * rows * panel * cols,
            bytes_accessed=4 * (panel * cols + rows * cols + rows * panel),
            transcendentals=0,
        ),
        name="contract",
    )(*(pieces[k] for k in keys), hi, lo, vir_pairs)


def shards(amplitudes, integrals, occ_pairs, vir_pairs):
    outer, inner, cores, slices = (lax.axis_size(a) for a in ("outer", "inner", "core", "ij"))
    per, panel = occ_pairs.shape[0], integrals.shape[0]
    own = pack(amplitudes, occ_pairs)
    far = [own] + [send(own, ("outer",), (d,)) for d in range(1, outer)]
    hi, lo = split_integrals(integrals)
    near = sort_slices(far, hi)
    pieces = {}
    for n, s in itertools.product(range(inner), range(slices)):
        piece = near[s]
        if n or s:
            piece = send(piece, ("inner", "ij"), (n, s))
        pieces[0, n, s] = piece
        for c in range(1, cores):
            pieces[c, n, s] = send(piece, ("core",), (c,))
    update = contract(pieces, hi, lo, vir_pairs[None, :], inner, cores)
    groups = outer * inner * cores
    update = update.reshape(groups, per, panel)
    moved = lax.all_to_all(
        update, ("outer", "inner", "core"), split_axis=0, concat_axis=0, tiled=True
    )
    return moved.transpose(1, 0, 2).reshape(per, groups * panel)


def solution(mesh):
    groups, slices = mesh.devices.shape
    cores = 2 if groups % 2 == 0 else 1
    chips = groups // cores
    outer = chips
    if is_power(chips):
        outer = 1 << (chips.bit_length() // 2)
    shape = (outer, chips // outer, cores, slices)
    ab = ("outer", "inner", "core")
    return jax.shard_map(
        shards,
        mesh=Mesh(mesh.devices.reshape(shape), (*ab, "ij")),
        in_specs=(P(ab, "ij"), P(ab, None), P((*ab, "ij")), P(ab)),
        out_specs=P((*ab, "ij"), None),
        check_vma=False,
    )
```
